32 devices in a mesh: groups: 2 (over x), wide: 16 (over z, y, core).
Axes of the slice: x: 2, y: 2, z: 4, core: 2. Of those that a mesh axis runs over, the one named last changes fastest.
Arguments:
- residual: bfloat16 [4096, 2048], P(('groups', 'wide')), parts along dimension 0, may hold values from -6 to 6
- queries: bfloat16 [4096, 2048], P(('groups', 'wide')), parts along dimension 0, may hold values from -160 to 160
- new_keys: bfloat16 [4096, 256], P(('groups', 'wide')), parts along dimension 0, may hold values from -6 to 6
- new_values: bfloat16 [4096, 256], P(('groups', 'wide')), parts along dimension 0, may hold values from -6 to 6
- cache_keys: bfloat16 [32, 2048, 256], P(('groups', 'wide')), parts along dimension 0, may hold values from -6 to 6
- cache_values: bfloat16 [32, 2048, 256], P(('groups', 'wide')), parts along dimension 0, may hold values from -6 to 6
- cache_len: int32 [32], P('groups'), parts along dimension 0, may hold values from 1 to 2048, 16384 in all
- o_weight: bfloat16 [2048, 2048], P('wide'), may hold values from -0.75 to 0.75
- norm_gain: float32 [2048], replicated, may hold values from 0.5 to 2
- expert_ids: int32 [4096, 8], P(('groups', 'wide')), parts along dimension 0, may hold values from 0 to 15, all different within a row; in each aligned block of 128 rows (0 to 127, 128 to 255, ...) at most 72 rows name the same one
- gate_raw: float32 [4096, 8], P(('groups', 'wide')), parts along dimension 0, may hold values from 0.1 to 1
- w_gate: bfloat16 [16, 2048, 768], P('wide'), may hold values from -0.125 to 0.125
- w_up: bfloat16 [16, 2048, 768], P('wide'), may hold values from -0.125 to 0.125
- w_down: bfloat16 [16, 768, 2048], P('wide'), may hold values from -0.4375 to 0.4375
Outputs:
- layer_out: bfloat16 [4096, 2048], P(('groups', 'wide')), parts along dimension 0
The draws below stay inside these ranges and needn't reach their ends.
There are 2 independent parts, one for each index of `groups`. The reference program is written for one: setup_inputs(seed, part) draws one part's arguments, and reference() takes and returns one part's arrays. A program takes and returns all parts, laid end to end along the dimension named above; an argument that names none is the same for every part. Nothing has to cross between parts.
Inputs may be any that keep to these rules, and one draw needn't show every extreme that they name: `cache_len`: each span's cache holds 1 or more positions; in every part some span has a full cache of 2048 positions and the lengths sum to 16384. `expert_ids`: each token names 8 different experts; among the 128 tokens of one span no expert is named more than 72 times, and in every draw some span names some expert exactly 72 times.
All inputs are finite; a program needn't handle non-finite values.
Results may differ from the reference program's by a relative error of at most 0.01.
Values may be sent and summed in bfloat16 or wider, within the bound.
A program may use at most 128 MiB of HBM per device.

```python
import math
import jax
import jax.numpy as jnp
import numpy as np
from jax import lax

D = 2048
HEADS = 16
KV_HEADS = 2
HEAD = 128
FF = 768
TOPK = 8
SPAN = 128
CACHE = 2048
EXPERTS = 16
TOKENS = 2048
CAP = 72
N_WIDE = 16


def attention_fields(key):
    cached = jnp.clip(jax.random.normal(jax.random.fold_in(key, 11), (N_WIDE, CACHE, KV_HEADS * HEAD), jnp.float32), -4.5, 4.5)
    fresh = jnp.clip(jax.random.normal(jax.random.fold_in(key, 12), (TOKENS, KV_HEADS * HEAD), jnp.float32), -6.0, 6.0)
    asked = jnp.clip(jax.random.normal(jax.random.fold_in(key, 13), (TOKENS, HEADS * HEAD), jnp.float32), -6.0, 6.0)
    return (cached, fresh, asked)


def draw_cache_keys(key, part):
    return attention_fields(key)[0].astype(jnp.bfloat16)


def draw_new_keys(key, part):
    return attention_fields(key)[1].astype(jnp.bfloat16)


def draw_queries(key, part):
    return attention_fields(key)[2].astype(jnp.bfloat16)


def shard_levels(key, dims, shards, smallest, top_value):
    factor_of = 1.0
    for dim, blocks in shards:
        steps = jax.random.uniform(jax.random.fold_in(jax.random.fold_in(key, 6), dim), (blocks,), jnp.float32, smallest / len(shards), top_value / len(shards))
        factor_of = factor_of * jnp.repeat(jnp.exp(steps), dims[dim] // blocks).reshape((-1,) + (1,) * (len(dims) - 1 - dim))
    return factor_of


def length_profile(amount, total, most, slope):
    loads = [(1 << 20) // math.isqrt(grade ** slope) + 1 for grade in range(2, amount + 1)]
    rest, given = total - most - (amount - 1), [1] * (amount - 1)
    while rest > 0:
        movable = [i for i in range(amount - 1) if given[i] < most]
        whole, budget = sum([loads[i] for i in movable]), rest
        for i in movable:
            addition = min(most - given[i], max(1, budget * loads[i] // whole), rest)
            given[i] = given[i] + addition
            rest = rest - addition
    return np.array([most] + given)


def uneven(key, number_of, total, bound, slope):
    if number_of == 2:
        one = jax.random.randint(key, (), max(1, total - bound), min(bound, total - 1) + 1)
        return jnp.stack([one, total - one])
    tallies = jnp.asarray(length_profile(number_of, total, bound, slope), jnp.int32)
    pairs = (number_of - 1) // 2
    source_of, receiver = tallies[1:1 + 2 * pairs:2], tallies[2:2 + 2 * pairs:2]
    room = jnp.minimum(source_of - 1, bound - receiver)
    passed = jax.random.randint(jax.random.fold_in(key, 1), (pairs,), 0, 1 << 20) % (room + 1)
    tallies = tallies.at[1:1 + 2 * pairs:2].set(source_of - passed).at[2:2 + 2 * pairs:2].set(receiver + passed)
    return tallies[jax.random.permutation(jax.random.fold_in(key, 2), number_of)]


def routed_block(rng, own, number, rows, amount, top, most, slope):
    order = jax.random.permutation(rng, amount)
    packed, usual = portions_of(amount, rows * top, most, slope, True), portions_of(amount, rows * top, most, slope, False)
    places = jnp.arange(amount)

    def named(sizes, turn):
        used = int((sizes > 0).sum())
        fixed = max(1, used // 4)
        moved = fixed + (places - fixed + turn * (used - fixed)) % max(1, amount - fixed)
        return jnp.zeros((amount,), jnp.int32).at[order[jnp.where(places < fixed, places, moved)]].set(jnp.asarray(sizes, jnp.int32))

    sizes = jnp.where(number % 4 == 0, named(packed, number // 4), named(usual, number - number // 4 - 1))
    mixed = jax.random.permutation(jax.random.fold_in(own, 3), amount)
    source_of, receiver = mixed[0:amount // 2 * 2:2], mixed[1:amount // 2 * 2:2]
    margin = jnp.minimum(sizes[source_of] - 1, most - sizes[receiver]) // 2
    margin = jnp.where((source_of == order[0]) | (receiver == order[0]) | (sizes[receiver] == 0), 0, jnp.maximum(margin, 0))
    moved = jax.random.randint(jax.random.fold_in(own, 4), (amount // 2,), 0, 1 << 20) % (margin + 1)
    sizes = sizes.at[source_of].add(-moved).at[receiver].add(moved)
    members = jnp.searchsorted(jnp.cumsum(sizes), jnp.arange(rows * top), side="right").astype(jnp.int32)
    grid = members.reshape(top, rows).T
    grid = grid[jax.random.permutation(jax.random.fold_in(own, 1), rows)]
    turn = jax.random.randint(jax.random.fold_in(own, 2), (rows, 1), 0, top)
    return jnp.take_along_axis(grid, (jnp.arange(top)[None, :] + turn) % top, axis=1)


def portions_of(count, total, reach, skew, full):
    weights = [(1 << 20) // math.isqrt(rank ** skew) + 1 for rank in range(1, count + 1)]
    largest = reach if full else min(reach, max(-(-total // count), total * weights[0] // sum(weights)))
    least = 1 if total - largest >= count - 1 else 0
    counts, rest = [largest] + [least] * (count - 1), total - largest - least * (count - 1)
    while rest > 0:
        free = [i for i in range(1, count) if counts[i] < largest] or [i for i in range(1, count) if counts[i] < reach]
        pool, budget = sum([weights[i] for i in free]), rest
        for i in free:
            addition = min(reach - counts[i], max(1, budget * weights[i] // pool), rest)
            counts[i] = counts[i] + addition
            rest = rest - addition
    return np.array(counts)


def gaussian(stream_key, dims, spread, limit, split=(), dtype=jnp.bfloat16):
    entries = jax.random.normal(stream_key, dims, jnp.float32) * spread
    if len(split) > 0:
        entries = shard_levels(stream_key, dims, split, -0.22, 0.18) * entries
    return jnp.clip(entries, min=-limit, max=limit).astype(dtype)


def setup_inputs(seed: int = 0, part: int = 0) -> dict:
    streams_of = jax.random.split(jax.random.key(seed), 15)
    part_keys = jax.random.split(jax.random.fold_in(streams_of[14], part), 15)
    residual = gaussian(part_keys[0], (TOKENS, D), 1.0, 6.0, ((0, 16),))
    queries = draw_queries(jax.random.fold_in(jax.random.fold_in(streams_of[14], part), 71), part)
    new_keys = draw_new_keys(jax.random.fold_in(jax.random.fold_in(streams_of[14], part), 71), part)
    new_values = gaussian(part_keys[3], (TOKENS, KV_HEADS * HEAD), 1.0, 6.0, ((0, 16),))
    cache_keys = draw_cache_keys(jax.random.fold_in(jax.random.fold_in(streams_of[14], part), 71), part)
    cache_values = gaussian(part_keys[5], (N_WIDE, CACHE, KV_HEADS * HEAD), 1.0, 6.0, ((0, 16),))
    cache_len = uneven(part_keys[6], N_WIDE, N_WIDE * CACHE // 2, CACHE, 2).astype(jnp.int32)
    o_weight = gaussian(streams_of[7], (HEADS * HEAD, D), (D // 32) ** -0.5, 0.75, ((0, 16),))
    norm_gain = jnp.clip(jnp.exp(jax.random.uniform(streams_of[8], (D,), jnp.float32, math.log(0.5), math.log(2.0))), 0.5, 2.0)
    expert_ids_keys = jax.random.split(jax.random.fold_in(part_keys[9], 1), TOKENS // SPAN)
    expert_ids_turns = jax.random.permutation(jax.random.fold_in(part_keys[9], 3), TOKENS // SPAN)
    expert_ids = jax.vmap(lambda own, number: routed_block(jax.random.fold_in(part_keys[9], 2), own, number, SPAN, EXPERTS, TOPK, CAP, 1))(expert_ids_keys, expert_ids_turns).reshape((TOKENS, TOPK))
    gate_raw = jnp.clip(jnp.exp(math.log(1.0) - 2.3025851 * jax.random.uniform(part_keys[10], (TOKENS, TOPK), jnp.float32) ** shard_levels(part_keys[10], (TOKENS, TOPK), ((0, 16),), -0.2, 0.2)), 0.1, 1.0)
    w_gate = gaussian(streams_of[11], (EXPERTS, D, FF), D ** -0.5, 0.125, ((0, 16),))
    w_up = gaussian(streams_of[12], (EXPERTS, D, FF), D ** -0.5, 0.125, ((0, 16),))
    w_down = gaussian(streams_of[13], (EXPERTS, FF, D), (FF // 4) ** -0.5, 0.4375, ((0, 16),))
    return {"residual": residual, "queries": queries, "new_keys": new_keys, "new_values": new_values, "cache_keys": cache_keys, "cache_values": cache_values, "cache_len": cache_len, "o_weight": o_weight, "norm_gain": norm_gain, "expert_ids": expert_ids, "gate_raw": gate_raw, "w_gate": w_gate, "w_up": w_up, "w_down": w_down}


def attend_span(inputs):
    query_rows, key_new, value_new, key_cache, value_cache, length = inputs
    group_size = HEADS // KV_HEADS
    query_four = query_rows.astype(jnp.float32).reshape(SPAN, KV_HEADS, group_size, HEAD)
    key_all = jnp.concatenate([key_cache, key_new], axis=0).astype(jnp.float32).reshape(CACHE + SPAN, KV_HEADS, HEAD)
    value_all = jnp.concatenate([value_cache, value_new], axis=0).astype(jnp.float32).reshape(CACHE + SPAN, KV_HEADS, HEAD)
    scores = jnp.einsum('tgrd,kgd->grtk', query_four, key_all) * HEAD ** (-0.5)
    positions = jnp.arange(CACHE + SPAN).astype(jnp.int32)
    token_rows = jnp.arange(SPAN).astype(jnp.int32)
    visible = jnp.where(positions[None, :] < CACHE, positions[None, :] < length, positions[None, :] - CACHE <= token_rows[:, None])
    scores = jnp.where(visible[None, None], scores, jnp.float32(-1e+30))
    row_max = lax.optimization_barrier(jnp.max(scores, axis=-1, keepdims=True))
    weights = jnp.exp(scores - row_max)
    denominator = lax.optimization_barrier(jnp.sum(weights, axis=-1))
    rounded = lax.optimization_barrier(weights.astype(jnp.bfloat16)).astype(jnp.float32)
    numerator = jnp.einsum('grtk,kgd->grtd', rounded, value_all)
    output = numerator / denominator[..., None]
    return jnp.transpose(output, (2, 0, 1, 3)).reshape(SPAN, HEADS * HEAD).astype(jnp.bfloat16)

def reference(residual, queries, new_keys, new_values, cache_keys, cache_values, cache_len, o_weight, norm_gain, expert_ids, gate_raw, w_gate, w_up, w_down):
    attn = lax.map(attend_span, (queries.reshape(N_WIDE, SPAN, HEADS * HEAD), new_keys.reshape(N_WIDE, SPAN, KV_HEADS * HEAD), new_values.reshape(N_WIDE, SPAN, KV_HEADS * HEAD), cache_keys, cache_values, cache_len))
    attn = attn.reshape(TOKENS, HEADS * HEAD)
    projected = jnp.dot(attn, o_weight, preferred_element_type=jnp.float32)
    mixed = residual.astype(jnp.float32) + projected
    normed = (mixed * lax.rsqrt(lax.optimization_barrier(jnp.mean(mixed * mixed, axis=-1, keepdims=True)) + 1e-06) * norm_gain).astype(jnp.bfloat16)
    shares = gate_raw / lax.optimization_barrier(jnp.sum(gate_raw, axis=-1, keepdims=True))
    flat_ids = expert_ids.reshape(N_WIDE, SPAN * TOPK)
    one_hot = (flat_ids[..., None] == jnp.arange(EXPERTS).astype(jnp.int32)[None, None, :]).astype(jnp.int32)
    ranks = (lax.optimization_barrier(jnp.sum(jnp.cumsum(one_hot, axis=1) * one_hot, axis=-1)) - 1).astype(jnp.int32)
    source = jnp.arange(N_WIDE).astype(jnp.int32)[:, None]
    destination = (flat_ids * (N_WIDE * CAP) + source * CAP + ranks).astype(jnp.int32).reshape(-1)
    global_tokens = (source * SPAN + (jnp.arange(SPAN * TOPK).astype(jnp.int32) // TOPK)[None, :]).astype(jnp.int32).reshape(-1)
    token_table = jnp.full((EXPERTS * N_WIDE * CAP,), TOKENS, jnp.int32).at[destination].set(global_tokens).reshape(EXPERTS, N_WIDE * CAP)
    share_table = jnp.zeros((EXPERTS * N_WIDE * CAP,), jnp.float32).at[destination].set(shares.reshape(-1)).reshape(EXPERTS, N_WIDE * CAP)
    padded = jnp.concatenate([normed, jnp.zeros((1, D), jnp.bfloat16)], axis=0)

    def expert_step(carry, inputs):
        table_row, share_row, gate_w, up_w, down_w = inputs
        rows_in = padded[table_row]
        gate_part = jnp.dot(rows_in, gate_w, preferred_element_type=jnp.float32)
        up_part = jnp.dot(rows_in, up_w, preferred_element_type=jnp.float32)
        activated = (jax.nn.silu(gate_part) * up_part).astype(jnp.bfloat16)
        expert_rows = jnp.dot(activated, down_w, preferred_element_type=jnp.float32).astype(jnp.bfloat16)
        carry = carry.at[table_row].add(expert_rows.astype(jnp.float32) * share_row[:, None])
        return (carry, None)
    routed, unused = lax.scan(expert_step, jnp.zeros((TOKENS + 1, D), jnp.float32), (token_table, share_table, w_gate, w_up, w_down))
    return (mixed + routed[:TOKENS]).astype(jnp.bfloat16)
```

```python
import functools
import jax
import jax.numpy as jnp
from jax import lax
from jax.experimental import pallas as pl
from jax.experimental.pallas import tpu as pltpu
from jax.sharding import PartitionSpec as P

D = 2048
HEADS = 16
KV_HEADS = 2
HEAD = 128
TOPK = 8
SPAN = 128
PACK = 2
EXP2_SCALE = HEAD ** (-0.5) * 1.4426950408889634
CHUNKS = 2


def attention_kernel(length_ref, q_ref, nk_ref, nv_ref, k_ref, v_ref, out_ref):
    tokens = q_ref.shape[0]
    rows = PACK * tokens
    cache = k_ref.shape[1]
    q = jnp.concatenate([q_ref[:, i * HEAD : (i + 1) * HEAD] for i in range(PACK)], axis=0)
    dims = (((1,), (1,)), ((), ()))
    s = lax.dot_general(q, k_ref[0], dims, preferred_element_type=jnp.float32)
    position = lax.broadcasted_iota(jnp.int32, (1, cache), 1)
    s = jnp.where(position < length_ref[0], s, jnp.float32(-1e30))
    s_new = lax.dot_general(q, nk_ref[...], dims, preferred_element_type=jnp.float32)
    row = lax.broadcasted_iota(jnp.int32, (rows, tokens), 0) % tokens
    column = lax.broadcasted_iota(jnp.int32, (rows, tokens), 1)
    s_new = jnp.where(column <= row, s_new, jnp.float32(-1e30))
    top = jnp.maximum(jnp.max(s, axis=1, keepdims=True), jnp.max(s_new, axis=1, keepdims=True))
    w = jnp.exp2((s - top) * EXP2_SCALE)
    w_new = jnp.exp2((s_new - top) * EXP2_SCALE)
    total = jnp.sum(w, axis=1, keepdims=True) + jnp.sum(w_new, axis=1, keepdims=True)
    out = jnp.dot(w.astype(jnp.bfloat16), v_ref[0], preferred_element_type=jnp.float32)
    out += jnp.dot(w_new.astype(jnp.bfloat16), nv_ref[...], preferred_element_type=jnp.float32)
    out = (out / total).astype(out_ref.dtype)
    for i in range(PACK):
        out_ref[:, i * HEAD : (i + 1) * HEAD] = out[i * tokens : (i + 1) * tokens]


def attention(length, queries, new_keys, new_values, cache_keys, cache_values):
    tokens, width = queries.shape
    cache = cache_keys.shape[1]
    per_group = HEADS // KV_HEADS // PACK
    return pl.pallas_call(
        attention_kernel,
        grid=(HEADS // PACK,),
        in_specs=[
            pl.BlockSpec(memory_space=pltpu.SMEM),
            pl.BlockSpec((tokens, PACK * HEAD), lambda i: (0, i)),
            pl.BlockSpec((tokens, HEAD), lambda i: (0, i // per_group)),
            pl.BlockSpec((tokens, HEAD), lambda i: (0, i // per_group)),
            pl.BlockSpec((1, cache, HEAD), lambda i: (0, 0, i // per_group)),
            pl.BlockSpec((1, cache, HEAD), lambda i: (0, 0, i // per_group)),
        ],
        out_specs=pl.BlockSpec((tokens, PACK * HEAD), lambda i: (0, i)),
        out_shape=jax.ShapeDtypeStruct((tokens, width), jnp.bfloat16),
        cost_estimate=pl.CostEstimate(
            flops=4 * tokens * width * (cache + tokens),
            bytes_accessed=4 * cache * KV_HEADS * HEAD + 4 * tokens * width,
            transcendentals=tokens * HEADS * (cache + tokens),
        ),
    )(length, queries, new_keys, new_values, cache_keys, cache_values)


def run_expert(rows_in, gate_w, up_w, down_w):
    gate_part = jnp.dot(rows_in, gate_w, preferred_element_type=jnp.float32)
    up_part = jnp.dot(rows_in, up_w, preferred_element_type=jnp.float32)
    activated = (jax.nn.silu(gate_part) * up_part).astype(jnp.bfloat16)
    return jnp.dot(activated, down_w, preferred_element_type=jnp.float32)


def sparse_experts(normed, expert_ids, shares, gate_w, up_w, down_w, devices):
    token_count = normed.shape[0]
    capacity = SPAN * TOPK // devices + max(2, SPAN * TOPK // (8 * devices))
    flat_ids = expert_ids.reshape(-1)
    one_hot = (flat_ids[:, None] == jnp.arange(devices, dtype=jnp.int32)[None, :]).astype(jnp.int32)
    ranks = jnp.sum(jnp.cumsum(one_hot, axis=0) * one_hot, axis=1) - 1
    slot_index = flat_ids * capacity + ranks
    token_of = jnp.arange(flat_ids.shape[0], dtype=jnp.int32) // TOPK
    slot_token = (
        jnp.full((devices * capacity,), token_count, jnp.int32).at[slot_index].set(token_of)
    )
    padded = jnp.concatenate([normed, jnp.zeros((1, D), jnp.bfloat16)], axis=0)
    outgoing = padded[slot_token].reshape(devices, capacity, D)
    arrived = lax.all_to_all(outgoing, "wide", split_axis=0, concat_axis=0, tiled=True)
    served = run_expert(arrived.reshape(-1, D), gate_w, up_w, down_w).astype(jnp.bfloat16)
    served = served.reshape(devices, capacity, D)
    returned_rows = lax.all_to_all(served, "wide", split_axis=0, concat_axis=0, tiled=True)
    picked = returned_rows.reshape(devices * capacity, D)[slot_index].reshape(token_count, TOPK, D)
    return jnp.sum(picked.astype(jnp.float32) * shares[..., None], axis=1)


def dense_experts(normed, expert_ids, shares, gate_w, up_w, down_w, devices):
    token_count = normed.shape[0]
    me = lax.axis_index("wide")
    hits = expert_ids[:, :, None] == jnp.arange(devices, dtype=jnp.int32)[None, None, :]
    share_of = jnp.sum(jnp.where(hits, shares[..., None], 0.0), axis=1)
    all_shares = lax.all_gather(share_of, "wide", axis=0, tiled=False)
    mine = lax.dynamic_index_in_dim(all_shares, me, axis=2, keepdims=False)
    size = token_count // CHUNKS
    parts = []
    for c in range(CHUNKS):
        piece = lax.slice_in_dim(normed, c * size, (c + 1) * size, axis=0)
        rows = lax.all_gather(piece, "wide", axis=0, tiled=True)
        out = run_expert(rows, gate_w, up_w, down_w)
        scale = mine[:, c * size : (c + 1) * size].reshape(-1, 1)
        scaled = (out * scale).astype(jnp.bfloat16)
        parts.append(lax.psum_scatter(scaled, "wide", scatter_dimension=0, tiled=True))
    return jnp.concatenate(parts, axis=0).astype(jnp.float32)


def per_device(
    residual,
    queries,
    new_keys,
    new_values,
    cache_keys,
    cache_values,
    cache_len,
    o_weight,
    norm_gain,
    expert_ids,
    gate_raw,
    w_gate,
    w_up,
    w_down,
):
    devices = lax.axis_size("wide")
    me = lax.axis_index("wide")
    length = lax.dynamic_slice_in_dim(cache_len, me, 1, 0)
    attn = attention(length, queries, new_keys, new_values, cache_keys, cache_values)
    projected = jnp.dot(
        attn,
        lax.all_gather(o_weight, "wide", axis=0, tiled=True),
        preferred_element_type=jnp.float32,
    )
    mixed = residual.astype(jnp.float32) + projected
    normed = (
        mixed * lax.rsqrt(jnp.mean(mixed * mixed, axis=-1, keepdims=True) + 1e-06) * norm_gain
    ).astype(jnp.bfloat16)
    shares = gate_raw / jnp.sum(gate_raw, axis=-1, keepdims=True)
    experts = dense_experts if devices <= 2 * TOPK else sparse_experts
    routed = experts(normed, expert_ids, shares, w_gate[0], w_up[0], w_down[0], devices)
    return (mixed + routed).astype(jnp.bfloat16)


def solution(mesh):
    rows = P(("groups", "wide"), None)
    blocks = P(("groups", "wide"), None, None)
    weights = P("wide", None, None)
    placed = (rows, rows, rows, rows, blocks, blocks, P("groups"), P("wide", None), P())
    placed += (rows, rows, weights, weights, weights)
    return jax.shard_map(
        per_device,
        mesh=mesh,
        in_specs=placed,
        out_specs=rows,
        check_vma=False,
    )
```
